32 devices in a mesh: grp: 2 (over y), head: 4 (over z), tm: 4 (over x, core).
Axes of the slice: x: 2, y: 2, z: 4, core: 2. Of those that a mesh axis runs over, the one named last changes fastest.
Arguments:
- query_rows: bfloat16 [32, 64, 3072], P(('grp', 'tm'), 'head'), parts along dimension 0, may hold values from -180 to 180
- key_rows: bfloat16 [32, 64, 3072], P(('grp', 'tm'), 'head'), parts along dimension 0, may hold values from -6 to 6
- value_rows: bfloat16 [32, 64, 3072], P(('grp', 'tm'), 'head'), parts along dimension 0, may hold values from -6 to 6
- pair_list: int32 [32, 32], P('grp'), parts along dimension 0, may hold values from 0 to 15, as said below
- block_tokens: int32 [32], P('grp'), parts along dimension 0, may hold values from 1 to 64, 768 in all
Outputs:
- attended: bfloat16 [32, 64, 3072], P(('grp', 'tm'), 'head'), parts along dimension 0
The draws below stay inside these ranges and needn't reach their ends.
There are 2 independent parts, one for each index of `grp`. The reference program is written for one: setup_inputs(seed, part) draws one part's arguments, and reference() takes and returns one part's arrays. A program takes and returns all parts, laid end to end along the dimension named above; each array names one. Nothing has to cross between parts.
Inputs may be any that keep to these rules, and one draw needn't show every extreme that they name: `pair_list`: row q names q in column 0 and q xor 1 in column 1; a block may be named twice in a row. The query blocks of one time shard name at most 2 different blocks of a time shard beside it and at most 1 of a time shard two or more away; both bounds are reached.
All inputs are finite; a program needn't handle non-finite values.
Results may differ from the reference program's by a relative error of at most 0.0012.
The reference program's roundings to bfloat16 on the way (of `query_rot`, `key_rot`, `value_rot` and `weights_half`) count: a program that leaves them out, or rounds other values in their place, can miss the bound.
Values may be sent and summed in bfloat16 or wider, within the bound.
A program may use at most 128 MiB of HBM per device.

```python
import math
import jax
import jax.numpy as jnp
import numpy as np
from jax import lax

HEADS = 24
HD = 128
BLK = 64
KPB = 32
NB_DEV = 4
NBLK = 16


def attention_inputs(key):
    base_key = jax.random.fold_in(key, 31)
    query_seed, key_seed = jax.random.split(base_key)
    query_all = jnp.clip(jax.random.normal(query_seed, (NBLK, BLK, HEADS, HD), jnp.float32), -6.0, 6.0)
    key_all = jnp.clip(jax.random.normal(key_seed, (NBLK, BLK, HEADS, HD), jnp.float32), -6.0, 6.0)
    return (query_all.reshape(NBLK, BLK, HEADS * HD), key_all.reshape(NBLK, BLK, HEADS * HD))


def draw_query_rows(key, part):
    return attention_inputs(key)[0].astype(jnp.bfloat16)


def draw_key_rows(key, part):
    return attention_inputs(key)[1].astype(jnp.bfloat16)


def draw_pair_list(key, part):
    seeds = jax.random.split(jax.random.fold_in(key, 47), 8)
    shards = NBLK // NB_DEV
    blocks = jnp.arange(NBLK, dtype=jnp.int32)
    owner = blocks // NB_DEV
    inside = blocks % NB_DEV
    first_pick = jax.random.randint(seeds[0], (shards, shards), 0, NB_DEV)
    step_pick = jax.random.randint(seeds[1], (shards, shards), 1, NB_DEV)
    second_pick = (first_pick + step_pick) % NB_DEV
    far_pick = jax.random.randint(seeds[2], (shards, shards), 0, NB_DEV)
    offsets = jax.random.randint(seeds[3], (NBLK, KPB - 12), -3, 4)
    local_cols = owner[:, None] * NB_DEV + jnp.clip(inside[:, None] + offsets, 0, NB_DEV - 1)
    upper = jnp.where(owner + 1 < shards, owner + 1, owner - 1)
    lower = jnp.where(owner >= 1, owner - 1, owner + 1)
    up_col = upper * NB_DEV + jnp.where(inside % 2 == 0, first_pick[owner, upper], second_pick[owner, upper])
    coin_flip = jax.random.randint(seeds[4], (NBLK,), 0, 2)
    low_col = lower * NB_DEV + jnp.where(coin_flip == 0, first_pick[owner, lower], second_pick[owner, lower])
    span_top = max(shards - 2, 1)
    dist_first = jax.random.randint(seeds[5], (NBLK, 8), 0, span_top)
    dist_second = jax.random.randint(seeds[6], (NBLK, 8), 0, span_top)
    reach = 2 + jnp.minimum(dist_first, dist_second)
    side_sign = jax.random.randint(seeds[7], (NBLK, 8), 0, 2) * 2 - 1
    target = owner[:, None] + side_sign * reach
    target = jnp.where((target >= 0) & (target < shards), target, owner[:, None] - side_sign * reach)
    usable = (target >= 0) & (target < shards)
    safe_target = jnp.clip(target, 0, shards - 1)
    owner_wide = jnp.broadcast_to(owner[:, None], (NBLK, 8))
    far_cols = jnp.where(usable, safe_target * NB_DEV + far_pick[owner_wide, safe_target], blocks[:, None])
    columns = [blocks[:, None], (blocks ^ 1)[:, None], local_cols, up_col[:, None], low_col[:, None], far_cols]
    return jnp.concatenate(columns, axis=1).astype(jnp.int32)


def block_levels(rng, extent, cuts, least, high):
    factor_of, own = 1.0, jax.random.fold_in(rng, 6)
    for axis_at, blocks in cuts:
        draws = jnp.exp(jax.random.uniform(jax.random.fold_in(own, axis_at), (blocks,), jnp.float32, least / len(cuts), high / len(cuts)))
        factor_of = factor_of * jnp.repeat(draws, extent[axis_at] // blocks).reshape([-1 if axis == axis_at else 1 for axis in range(len(extent))])
    return factor_of


def length_profile(number_of, total, most, skew):
    weights = [(1 << 20) // math.isqrt(rank ** skew) + 1 for rank in range(2, number_of + 1)]
    rest, holding = total - most - (number_of - 1), [1] * (number_of - 1)
    while rest > 0:
        candidates = [i for i in range(number_of - 1) if holding[i] < most]
        pool, budget = sum([weights[i] for i in candidates]), rest
        for i in candidates:
            extra = min(most - holding[i], max(1, budget * weights[i] // pool), rest)
            holding[i] = holding[i] + extra
            rest = rest - extra
    return np.array([most] + holding)


def ragged(own_key, count, total, bound, slope):
    if count == 2:
        one = jax.random.randint(own_key, (), max(1, total - bound), min(bound, total - 1) + 1)
        return jnp.stack([one, total - one])
    sizes = jnp.asarray(length_profile(count, total, bound, slope), jnp.int32)
    couples = (count - 1) // 2
    donor, receiver = sizes[1:1 + 2 * couples:2], sizes[2:2 + 2 * couples:2]
    margin = jnp.minimum(donor - 1, bound - receiver)
    moved = jax.random.randint(jax.random.fold_in(own_key, 1), (couples,), 0, 1 << 20) % (margin + 1)
    sizes = sizes.at[1:1 + 2 * couples:2].set(donor - moved).at[2:2 + 2 * couples:2].set(receiver + moved)
    return sizes[jax.random.permutation(jax.random.fold_in(own_key, 2), count)]


def bell_draw(own_key, dims, deviation, most, cuts=(), held_as=jnp.bfloat16):
    drawn = jax.random.normal(own_key, dims, jnp.float32) * deviation
    if len(cuts) > 0:
        drawn = block_levels(own_key, dims, cuts, -0.22, 0.18) * drawn
    return jnp.clip(drawn, min=-most, max=most).astype(held_as)


def setup_inputs(seed: int = 0, part: int = 0) -> dict:
    key_list = jax.random.split(jax.random.key(seed), 6)
    part_keys = jax.random.split(jax.random.fold_in(key_list[5], part), 6)
    query_rows = draw_query_rows(jax.random.fold_in(jax.random.fold_in(key_list[5], part), 71), part)
    key_rows = draw_key_rows(jax.random.fold_in(jax.random.fold_in(key_list[5], part), 71), part)
    value_rows = bell_draw(part_keys[2], (NBLK, BLK, HEADS * HD), 1.0, 6.0, ((0, 4), (1, 4)))
    pair_list = draw_pair_list(jax.random.fold_in(jax.random.fold_in(key_list[5], part), 71), part)
    block_tokens = ragged(part_keys[4], NBLK, NBLK * BLK * 3 // 4, BLK, 2).astype(jnp.int32)
    return {"query_rows": query_rows, "key_rows": key_rows, "value_rows": value_rows, "pair_list": pair_list, "block_tokens": block_tokens}


def sign_table(dimension):
    indices = jnp.arange(dimension, dtype=jnp.int32)
    common = indices[:, None] & indices[None, :]
    parity = jnp.zeros((dimension, dimension), jnp.int32)
    for bit_level in range(dimension.bit_length() - 1):
        parity = parity + (common >> bit_level & 1)
    return jnp.where(parity % 2 == 0, 1.0, -1.0).astype(jnp.float32)

def reference(query_rows, key_rows, value_rows, pair_list, block_tokens):
    sign_rows = sign_table(HD)
    sign_half = sign_rows.astype(jnp.bfloat16)
    rotate_scale = 1.0 / math.sqrt(HD)
    score_scale = 1.0 / math.sqrt(HD)

    def rotate(source):
        flattened = source.reshape(-1, HD)
        turned = jnp.dot(flattened, sign_half, preferred_element_type=jnp.float32) * rotate_scale
        return turned.astype(jnp.bfloat16).reshape(NBLK, BLK, HEADS, HD)
    query_rot = rotate(query_rows)
    key_rot = rotate(key_rows)
    value_rot = rotate(value_rows)
    positions = jnp.arange(BLK, dtype=jnp.int32)
    live_keys = positions[None, :] < block_tokens[:, None]
    earlier = jnp.arange(KPB)[:, None] > jnp.arange(KPB)[None, :]

    def one_block(block_id):
        listed = pair_list[block_id]
        repeated = jnp.any((listed[:, None] == listed[None, :]) & earlier, axis=1)
        key_keep = (live_keys[listed] & ~repeated[:, None]).reshape(KPB * BLK)
        key_block = key_rot[listed].reshape(KPB * BLK, HEADS, HD).astype(jnp.float32)
        value_block = value_rot[listed].reshape(KPB * BLK, HEADS, HD).astype(jnp.float32)
        query_block = query_rot[block_id].astype(jnp.float32)
        scores = jnp.einsum('qhd,khd->hqk', query_block, key_block) * score_scale
        scores = jnp.where(key_keep[None, None, :], scores, -1e+30)
        row_peak = lax.optimization_barrier(jnp.max(scores, axis=-1, keepdims=True))
        weights = jnp.exp(scores - row_peak)
        denominator = lax.optimization_barrier(jnp.sum(weights, axis=-1))
        weights_half = lax.optimization_barrier(weights.astype(jnp.bfloat16)).astype(jnp.float32)
        mixed_rows = jnp.einsum('hqk,khd->qhd', weights_half, value_block)
        mixed_rows = mixed_rows / jnp.transpose(denominator)[:, :, None]
        turned = jnp.dot(mixed_rows.reshape(-1, HD), sign_rows, precision=lax.Precision.HIGHEST) * rotate_scale
        turned = turned.reshape(BLK, HEADS * HD)
        live_rows = positions[:, None] < block_tokens[block_id]
        return jnp.where(live_rows, turned, 0.0).astype(jnp.bfloat16)
    return lax.map(one_block, jnp.arange(NBLK, dtype=jnp.int32))
```

```python
import functools
import math

import jax
import jax.numpy as jnp
from jax import lax
from jax.experimental import pallas as pl
from jax.experimental.pallas import tpu as pltpu
from jax.sharding import PartitionSpec as P

HD = 128
NEAR_CAP = 2
FAR_CAP = 1
LANES = 128
MESH = pl.DeviceIdType.MESH


def incoming_slots(count_tm):
    slots = []
    for offset in range(1, count_tm):
        capacity = NEAR_CAP if offset in (1, count_tm - 1) else FAR_CAP
        slots += [(offset, place) for place in range(capacity)]
    return slots


def sign_table(dimension):
    rows = lax.broadcasted_iota(jnp.int32, (dimension, dimension), 0)
    columns = lax.broadcasted_iota(jnp.int32, (dimension, dimension), 1)
    common = rows & columns
    parity = jnp.zeros((dimension, dimension), jnp.int32)
    for bit_level in range(dimension.bit_length() - 1):
        parity = parity + ((common >> bit_level) & 1)
    return jnp.where((parity & 1) == 0, 1.0, -1.0).astype(jnp.float32)


def kernel(
    sizes,
    query_ref,
    key_ref,
    value_ref,
    pair_ref,
    tokens_ref,
    out_ref,
    gathered,
    store,
    outbox,
    staged,
    pair_here,
    listed_ref,
    place_ref,
    wanted_ref,
    bias_ref,
    sign_ref,
    head_send,
    head_recv,
    local_sem,
    halo_send,
    halo_recv,
    back_send,
    back_recv,
    back_local,
    pair_sem,
):
    count_head, count_tm, blocks, part, heads, block, total_blocks, slots, padded = sizes
    width = heads * HD
    my_head = lax.axis_index("head")
    me = lax.axis_index("tm")
    scale = 1.0 / math.sqrt(HD)
    slot_of = {slot: i for i, slot in enumerate(slots)}
    sources = (key_ref, value_ref, query_ref)

    for offset in range(1, count_head):
        peer = lax.rem(my_head + offset, count_head)
        pl.semaphore_signal(
            pltpu.get_barrier_semaphore(), inc=1, device_id={"head": peer}, device_id_type=MESH
        )

    def columns_of(owner, h):
        return pl.ds(pl.multiple_of(owner * width + h * HD, HD), HD)

    def head_copy(which, offset, h):
        peer = lax.rem(my_head + offset, count_head)
        return pltpu.make_async_remote_copy(
            src_ref=sources[which].at[:, :, columns_of(peer, h)],
            dst_ref=gathered.at[which, h, my_head],
            send_sem=head_send.at[which, offset - 1, h],
            recv_sem=head_recv.at[which, offset - 1, h],
            device_id={"head": peer},
            device_id_type=MESH,
        )

    def local_copy(which, h):
        return pltpu.make_async_copy(
            sources[which].at[:, :, columns_of(my_head, h)],
            gathered.at[which, h, my_head],
            local_sem.at[which, h],
        )

    def halo_copy(which, h, slot):
        offset, place = slot
        peer = lax.rem(me + offset, count_tm)
        landing = slot_of[(count_tm - offset, place)]
        return pltpu.make_async_remote_copy(
            src_ref=outbox.at[which, h, slot_of[slot]],
            dst_ref=store.at[which, h, blocks + landing],
            send_sem=halo_send.at[which, h, slot_of[slot]],
            recv_sem=halo_recv.at[which, h, landing],
            device_id={"tm": peer},
            device_id_type=MESH,
        )

    def halo_arrival(which, h, slot):
        i = slot_of[slot]
        peer = lax.rem(me + slot[0], count_tm)
        return pltpu.make_async_remote_copy(
            src_ref=outbox.at[which, h, i],
            dst_ref=store.at[which, h, blocks + i],
            send_sem=halo_send.at[which, h, i],
            recv_sem=halo_recv.at[which, h, i],
            device_id={"tm": peer},
            device_id_type=MESH,
        )

    def if_used(slot, action):
        if slot[1] < FAR_CAP:
            action()
        else:
            peer = lax.rem(me + slot[0], count_tm)
            near = (peer == me + 1) | (peer == me - 1)
            pl.when(near)(action)

    def back_copy(offset, h):
        peer = lax.rem(my_head + offset, count_head)
        return pltpu.make_async_remote_copy(
            src_ref=staged.at[h, peer],
            dst_ref=out_ref.at[:, :, columns_of(my_head, h)],
            send_sem=back_send.at[offset - 1, h],
            recv_sem=back_recv.at[offset - 1, h],
            device_id={"head": peer},
            device_id_type=MESH,
        )

    def back_own(h):
        return pltpu.make_async_copy(
            staged.at[h, my_head],
            out_ref.at[:, :, columns_of(my_head, h)],
            back_local.at[h],
        )

    store[:, :, blocks:] = jnp.zeros((2, heads, padded - blocks, block, HD), jnp.bfloat16)
    for offset in range(1, count_tm):
        peer = lax.rem(me + offset, count_tm)
        pl.semaphore_signal(
            pltpu.get_barrier_semaphore(), inc=1, device_id={"tm": peer}, device_id_type=MESH
        )
    pair_copy = pltpu.make_async_copy(pair_ref, pair_here, pair_sem)
    pair_copy.start()
    for which in range(3):

        def start_local(h, carry, which=which):
            local_copy(which, h).start()
            return carry

        lax.fori_loop(0, heads, start_local, 0)
    sign_ref[...] = sign_table(HD).astype(jnp.bfloat16)
    pl.semaphore_wait(pltpu.get_barrier_semaphore(), count_head - 1 + count_tm - 1)
    for which in range(3):

        def start_remote(h, carry, which=which):
            for offset in range(1, count_head):
                head_copy(which, offset, h).start()
            return carry

        lax.fori_loop(0, heads, start_remote, 0)

    pair_copy.wait()
    pairs = pair_here[...]
    lane = lax.broadcasted_iota(jnp.int32, (1, LANES), 1)
    listed = jnp.zeros((total_blocks, LANES), jnp.float32)
    token_row = jnp.zeros((1, LANES), jnp.float32)
    for k in range(total_blocks):
        found = jnp.max(jnp.where(pairs == k, 1.0, 0.0), axis=1, keepdims=True)
        here = jnp.where(lane == k, 1.0, 0.0)
        listed = listed + found * here
        token_row = token_row + here * tokens_ref[k].astype(jnp.float32)
    wanted_ref[...] = jnp.zeros_like(wanted_ref)
    for t in range(count_tm):
        of_shard = listed[t * blocks : (t + 1) * blocks]
        listed_ref[t] = of_shard
        wanted_ref[t : t + 1, :] = jnp.max(of_shard, axis=0, keepdims=True)
    low = lax.broadcasted_iota(jnp.int32, (LANES, LANES), 0)
    high = lax.broadcasted_iota(jnp.int32, (LANES, LANES), 1)
    low_shard, high_shard = jnp.zeros_like(low), jnp.zeros_like(high)
    lane_shard = jnp.zeros_like(lane)
    for t in range(1, count_tm):
        low_shard = low_shard + jnp.where(low >= t * blocks, 1, 0)
        high_shard = high_shard + jnp.where(high >= t * blocks, 1, 0)
        lane_shard = lane_shard + jnp.where(lane >= t * blocks, 1, 0)
    before = jnp.where((low_shard == high_shard) & (low < high), 1.0, 0.0).astype(jnp.bfloat16)
    wanted = wanted_ref[...]
    rank = jnp.dot(wanted.astype(jnp.bfloat16), before, preferred_element_type=jnp.float32)
    for place in range(NEAR_CAP):
        chosen = jnp.where(rank == float(place), wanted, 0.0)
        for t in range(count_tm):
            place_ref[place, t] = chosen[t : t + 1, :]
    picks = []
    for offset, place in slots:
        row = place_ref[place, lax.rem(me + offset, count_tm)]
        picks.append(
            [
                jnp.sum(jnp.where(lane == me * blocks + j, row, 0.0), axis=1, keepdims=True)
                for j in range(blocks)
            ]
        )
    mine = listed_ref[me]
    key_lane = lax.broadcasted_iota(jnp.int32, (1, padded * block), 1)
    key_end = jnp.zeros((blocks, padded * block), jnp.float32)
    for i in range(blocks + len(slots)):
        if i < blocks:
            kept_tokens = jnp.where(lane == me * blocks + i, token_row, 0.0)
        else:
            offset, place = slots[i - blocks]
            owner = lax.rem(me + offset, count_tm)
            row = place_ref[place, me]
            kept_tokens = jnp.where(lane_shard == owner, row * token_row, 0.0)
        kept = jnp.sum(mine * kept_tokens, axis=1, keepdims=True)
        inside = jnp.where((key_lane >= i * block) & (key_lane < (i + 1) * block), 1.0, 0.0)
        key_end = key_end + inside * (kept + float(i * block))
    bias_ref[...] = jnp.where(key_lane.astype(jnp.float32) < key_end, 0.0, -1e30)

    def arrived(which, h):
        local_copy(which, h).wait()
        for offset in range(1, count_head):
            head_copy(which, offset, h).wait_recv()
        rows = jnp.concatenate(
            [
                gathered[which, h, :, b].astype(jnp.float32).reshape(block, HD)
                for b in range(blocks)
            ],
            axis=0,
        ).astype(jnp.bfloat16)
        turned = jnp.dot(rows, sign_ref[...], preferred_element_type=jnp.float32) * scale
        return turned.astype(jnp.bfloat16)

    for which in range(2):

        def spread(h, carry, which=which):
            turned = arrived(which, h)
            store[which, h, 0:blocks] = turned.reshape(blocks, block, HD)
            wide = turned.astype(jnp.float32)
            for i, slot in enumerate(slots):
                sent = picks[i][0] * wide[0:block]
                for j in range(1, blocks):
                    sent = sent + picks[i][j] * wide[j * block : (j + 1) * block]
                outbox[which, h, i] = sent.astype(jnp.bfloat16)
            for slot in slots:
                if_used(slot, lambda slot=slot: halo_copy(which, h, slot).start())
            return carry

        lax.fori_loop(0, heads, spread, 0)

    position = lax.broadcasted_iota(jnp.int32, (block, HD), 0)

    def attend(h, carry):
        query = arrived(2, h)
        for which in range(2):
            for slot in slots:
                if_used(slot, lambda slot=slot, which=which: halo_arrival(which, h, slot).wait_recv())
        keys = store[0, h].reshape(padded * block, HD)
        values = store[1, h].reshape(padded * block, HD)
        mixed = []
        for b in range(blocks):
            scores = lax.dot_general(
                query[b * block : (b + 1) * block],
                keys,
                (((1,), (1,)), ((), ())),
                preferred_element_type=jnp.float32,
            )
            scores = scores * scale + bias_ref[b : b + 1, :]
            peak = jnp.max(scores, axis=1, keepdims=True)
            weights = jnp.exp(scores - peak)
            denominator = jnp.sum(weights, axis=1, keepdims=True)
            total = jnp.dot(
                weights.astype(jnp.bfloat16), values, preferred_element_type=jnp.float32
            )
            mixed.append(total / denominator)
        mixed = jnp.concatenate(mixed, axis=0)
        first = mixed.astype(jnp.bfloat16)
        rest = mixed - first.astype(jnp.float32)
        second = rest.astype(jnp.bfloat16)
        third = (rest - second.astype(jnp.float32)).astype(jnp.bfloat16)
        sign = sign_ref[...]
        turned = jnp.dot(first, sign, preferred_element_type=jnp.float32)
        turned = turned + jnp.dot(second, sign, preferred_element_type=jnp.float32)
        turned = turned + jnp.dot(third, sign, preferred_element_type=jnp.float32)
        turned = turned * scale
        for b in range(blocks):
            live = position < tokens_ref[me * blocks + b]
            result = jnp.where(live, turned[b * block : (b + 1) * block], 0.0)
            for owner in range(count_head):
                staged[h, owner, b] = result[owner * part : (owner + 1) * part].astype(jnp.bfloat16)
        for offset in range(1, count_head):
            back_copy(offset, h).start()
        back_own(h).start()
        return carry

    lax.fori_loop(0, heads, attend, 0)

    def finish(h, carry):
        for which in range(3):
            for offset in range(1, count_head):
                head_copy(which, offset, h).wait_send()
        for which in range(2):
            for slot in slots:
                if_used(slot, lambda slot=slot, which=which: halo_copy(which, h, slot).wait_send())
        for offset in range(1, count_head):
            back_copy(offset, h).wait()
        back_own(h).wait()
        return carry

    lax.fori_loop(0, heads, finish, 0)


def shards(query_rows, key_rows, value_rows, pair_list, block_tokens):
    count_head = lax.axis_size("head")
    count_tm = lax.axis_size("tm")
    blocks, part, full_width = query_rows.shape
    block = part * count_head
    heads = full_width // (HD * count_head)
    total_blocks, listed = pair_list.shape
    slots = incoming_slots(count_tm)
    filled = blocks + len(slots)
    per_lane_tile = max(1, LANES // block)
    padded = -(-filled // per_lane_tile) * per_lane_tile
    shard_rows = -(-count_tm // 8) * 8
    sizes = (count_head, count_tm, blocks, part, heads, block, total_blocks, slots, padded)
    peers = max(1, count_head - 1)
    anywhere = pl.BlockSpec(memory_space=pl.ANY)
    dma = pltpu.SemaphoreType.DMA
    return pl.pallas_call(
        functools.partial(kernel, sizes),
        out_shape=jax.ShapeDtypeStruct(query_rows.shape, jnp.bfloat16),
        in_specs=[anywhere] * 4 + [pl.BlockSpec(memory_space=pltpu.SMEM)],
        out_specs=anywhere,
        scratch_shapes=[
            pltpu.VMEM((3, heads, count_head, blocks, part, HD), jnp.bfloat16),
            pltpu.VMEM((2, heads, padded, block, HD), jnp.bfloat16),
            pltpu.VMEM((2, heads, len(slots), block, HD), jnp.bfloat16),
            pltpu.VMEM((heads, count_head, blocks, part, HD), jnp.bfloat16),
            pltpu.VMEM((total_blocks, listed), jnp.int32),
            pltpu.VMEM((count_tm, blocks, LANES), jnp.float32),
            pltpu.VMEM((NEAR_CAP, count_tm, 1, LANES), jnp.float32),
            pltpu.VMEM((shard_rows, LANES), jnp.float32),
            pltpu.VMEM((blocks, padded * block), jnp.float32),
            pltpu.VMEM((HD, HD), jnp.bfloat16),
            dma((3, peers, heads)),
            dma((3, peers, heads)),
            dma((3, heads)),
            dma((2, heads, len(slots))),
            dma((2, heads, len(slots))),
            dma((peers, heads)),
            dma((peers, heads)),
            dma((heads,)),
            dma(()),
        ],
        compiler_params=pltpu.CompilerParams(
            collective_id=0, has_side_effects=True, vmem_limit_bytes=32 * 1024 * 1024
        ),
    )(query_rows, key_rows, value_rows, pair_list, block_tokens)


def solution(mesh):
    placed = (
        P(("grp", "tm"), "head", None),
        P(("grp", "tm"), "head", None),
        P(("grp", "tm"), "head", None),
        P("grp", None),
        P("grp"),
    )
    return jax.shard_map(
        shards,
        mesh=mesh,
        in_specs=placed,
        out_specs=P(("grp", "tm"), "head", None),
        check_vma=False,
    )
```

```python
import functools
import math

import jax
import jax.numpy as jnp
from jax import lax
from jax.experimental import pallas as pl
from jax.experimental.pallas import tpu as pltpu
from jax.sharding import PartitionSpec as P

HD = 128
NEAR_CAP = 2
FAR_CAP = 1
LANES = 128
MESH = pl.DeviceIdType.MESH


def incoming_slots(count_tm):
    slots = []
    for offset in range(1, count_tm):
        capacity = NEAR_CAP if offset in (1, count_tm - 1) else FAR_CAP
        slots += [(offset, place) for place in range(capacity)]
    return slots


def sign_table(dimension):
    rows = lax.broadcasted_iota(jnp.int32, (dimension, dimension), 0)
    columns = lax.broadcasted_iota(jnp.int32, (dimension, dimension), 1)
    common = rows & columns
    parity = jnp.zeros((dimension, dimension), jnp.int32)
    for bit_level in range(dimension.bit_length() - 1):
        parity = parity + ((common >> bit_level) & 1)
    return jnp.where((parity & 1) == 0, 1.0, -1.0).astype(jnp.float32)


def kernel(
    sizes,
    query_ref,
    key_ref,
    value_ref,
    pair_ref,
    tokens_far,
    out_ref,
    gathered,
    store,
    outbox,
    staged,
    pair_here,
    tokens_ref,
    listed_ref,
    place_ref,
    wanted_ref,
    bias_ref,
    sign_ref,
    head_send,
    head_recv,
    local_sem,
    halo_send,
    halo_recv,
    back_send,
    back_recv,
    back_local,
    pair_sem,
    tokens_sem,
):
    count_head, count_tm, blocks, part, heads, block, total_blocks, slots, padded = sizes
    width = heads * HD
    my_head = lax.axis_index("head")
    me = lax.axis_index("tm")
    scale = 1.0 / math.sqrt(HD)
    slot_of = {slot: i for i, slot in enumerate(slots)}
    sources = (key_ref, value_ref, query_ref)

    for offset in range(1, count_head):
        peer = lax.rem(my_head + offset, count_head)
        pl.semaphore_signal(
            pltpu.get_barrier_semaphore(), inc=1, device_id={"head": peer}, device_id_type=MESH
        )

    def columns_of(owner, h):
        return pl.ds(pl.multiple_of(owner * width + h * HD, HD), HD)

    def head_copy(which, offset, h):
        peer = lax.rem(my_head + offset, count_head)
        return pltpu.make_async_remote_copy(
            src_ref=sources[which].at[:, :, columns_of(peer, h)],
            dst_ref=gathered.at[which, h, my_head],
            send_sem=head_send.at[which, offset - 1, h],
            recv_sem=head_recv.at[which, offset - 1, h],
            device_id={"head": peer},
            device_id_type=MESH,
        )

    def local_copy(which, h):
        return pltpu.make_async_copy(
            sources[which].at[:, :, columns_of(my_head, h)],
            gathered.at[which, h, my_head],
            local_sem.at[which, h],
        )

    def halo_copy(which, h, slot):
        offset, place = slot
        peer = lax.rem(me + offset, count_tm)
        landing = slot_of[(count_tm - offset, place)]
        return pltpu.make_async_remote_copy(
            src_ref=outbox.at[which, h, slot_of[slot]],
            dst_ref=store.at[which, h, blocks + landing],
            send_sem=halo_send.at[which, h, slot_of[slot]],
            recv_sem=halo_recv.at[which, h, landing],
            device_id={"tm": peer},
            device_id_type=MESH,
        )

    def halo_arrival(which, h, slot):
        i = slot_of[slot]
        peer = lax.rem(me + slot[0], count_tm)
        return pltpu.make_async_remote_copy(
            src_ref=outbox.at[which, h, i],
            dst_ref=store.at[which, h, blocks + i],
            send_sem=halo_send.at[which, h, i],
            recv_sem=halo_recv.at[which, h, i],
            device_id={"tm": peer},
            device_id_type=MESH,
        )

    def if_used(slot, action):
        if slot[1] < FAR_CAP:
            action()
        else:
            peer = lax.rem(me + slot[0], count_tm)
            near = (peer == me + 1) | (peer == me - 1)
            pl.when(near)(action)

    def back_copy(offset, h):
        peer = lax.rem(my_head + offset, count_head)
        return pltpu.make_async_remote_copy(
            src_ref=staged.at[h, peer],
            dst_ref=out_ref.at[:, :, columns_of(my_head, h)],
            send_sem=back_send.at[offset - 1, h],
            recv_sem=back_recv.at[offset - 1, h],
            device_id={"head": peer},
            device_id_type=MESH,
        )

    def back_own(h):
        return pltpu.make_async_copy(
            staged.at[h, my_head],
            out_ref.at[:, :, columns_of(my_head, h)],
            back_local.at[h],
        )

    store[:, :, blocks:] = jnp.zeros((2, heads, padded - blocks, block, HD), jnp.bfloat16)
    for offset in range(1, count_tm):
        peer = lax.rem(me + offset, count_tm)
        pl.semaphore_signal(
            pltpu.get_barrier_semaphore(), inc=1, device_id={"tm": peer}, device_id_type=MESH
        )
    pair_copy = pltpu.make_async_copy(pair_ref, pair_here, pair_sem)
    pair_copy.start()
    tokens_copy = pltpu.make_async_copy(tokens_far, tokens_ref, tokens_sem)
    tokens_copy.start()
    for which in range(3):

        def start_local(h, carry, which=which):
            local_copy(which, h).start()
            return carry

        lax.fori_loop(0, heads, start_local, 0)
    sign_ref[...] = sign_table(HD).astype(jnp.bfloat16)
    pl.semaphore_wait(pltpu.get_barrier_semaphore(), count_head - 1 + count_tm - 1)
    for which in range(3):

        def start_remote(h, carry, which=which):
            for offset in range(1, count_head):
                head_copy(which, offset, h).start()
            return carry

        lax.fori_loop(0, heads, start_remote, 0)

    pair_copy.wait()
    tokens_copy.wait()
    pairs = pair_here[...]
    lane = lax.broadcasted_iota(jnp.int32, (1, LANES), 1)
    listed = jnp.zeros((total_blocks, LANES), jnp.float32)
    token_row = jnp.zeros((1, LANES), jnp.float32)
    for k in range(total_blocks):
        found = jnp.max(jnp.where(pairs == k, 1.0, 0.0), axis=1, keepdims=True)
        here = jnp.where(lane == k, 1.0, 0.0)
        listed = listed + found * here
        token_row = token_row + here * tokens_ref[k].astype(jnp.float32)
    wanted_ref[...] = jnp.zeros_like(wanted_ref)
    for t in range(count_tm):
        of_shard = listed[t * blocks : (t + 1) * blocks]
        listed_ref[t] = of_shard
        wanted_ref[t : t + 1, :] = jnp.max(of_shard, axis=0, keepdims=True)
    low = lax.broadcasted_iota(jnp.int32, (LANES, LANES), 0)
    high = lax.broadcasted_iota(jnp.int32, (LANES, LANES), 1)
    low_shard, high_shard = jnp.zeros_like(low), jnp.zeros_like(high)
    lane_shard = jnp.zeros_like(lane)
    for t in range(1, count_tm):
        low_shard = low_shard + jnp.where(low >= t * blocks, 1, 0)
        high_shard = high_shard + jnp.where(high >= t * blocks, 1, 0)
        lane_shard = lane_shard + jnp.where(lane >= t * blocks, 1, 0)
    before = jnp.where((low_shard == high_shard) & (low < high), 1.0, 0.0).astype(jnp.bfloat16)
    wanted = wanted_ref[...]
    rank = jnp.dot(wanted.astype(jnp.bfloat16), before, preferred_element_type=jnp.float32)
    for place in range(NEAR_CAP):
        chosen = jnp.where(rank == float(place), wanted, 0.0)
        for t in range(count_tm):
            place_ref[place, t] = chosen[t : t + 1, :]
    picks = []
    for offset, place in slots:
        row = place_ref[place, lax.rem(me + offset, count_tm)]
        picks.append(
            [
                jnp.sum(jnp.where(lane == me * blocks + j, row, 0.0), axis=1, keepdims=True)
                for j in range(blocks)
            ]
        )
    mine = listed_ref[me]
    key_lane = lax.broadcasted_iota(jnp.int32, (1, padded * block), 1)
    key_end = jnp.zeros((blocks, padded * block), jnp.float32)
    for i in range(blocks + len(slots)):
        if i < blocks:
            kept_tokens = jnp.where(lane == me * blocks + i, token_row, 0.0)
        else:
            offset, place = slots[i - blocks]
            owner = lax.rem(me + offset, count_tm)
            row = place_ref[place, me]
            kept_tokens = jnp.where(lane_shard == owner, row * token_row, 0.0)
        kept = jnp.sum(mine * kept_tokens, axis=1, keepdims=True)
        inside = jnp.where((key_lane >= i * block) & (key_lane < (i + 1) * block), 1.0, 0.0)
        key_end = key_end + inside * (kept + float(i * block))
    bias_ref[...] = jnp.where(key_lane.astype(jnp.float32) < key_end, 0.0, -1e30)

    def arrived(which, h):
        local_copy(which, h).wait()
        for offset in range(1, count_head):
            head_copy(which, offset, h).wait_recv()
        rows = jnp.concatenate(
            [
                gathered[which, h, :, b].astype(jnp.float32).reshape(block, HD)
                for b in range(blocks)
            ],
            axis=0,
        ).astype(jnp.bfloat16)
        turned = jnp.dot(rows, sign_ref[...], preferred_element_type=jnp.float32) * scale
        return turned.astype(jnp.bfloat16)

    for which in range(2):

        def spread(h, carry, which=which):
            turned = arrived(which, h)
            store[which, h, 0:blocks] = turned.reshape(blocks, block, HD)
            wide = turned.astype(jnp.float32)
            for i, slot in enumerate(slots):
                sent = picks[i][0] * wide[0:block]
                for j in range(1, blocks):
                    sent = sent + picks[i][j] * wide[j * block : (j + 1) * block]
                outbox[which, h, i] = sent.astype(jnp.bfloat16)
            for slot in slots:
                if_used(slot, lambda slot=slot: halo_copy(which, h, slot).start())
            return carry

        lax.fori_loop(0, heads, spread, 0)

    position = lax.broadcasted_iota(jnp.int32, (block, HD), 0)

    def attend(h, carry):
        query = arrived(2, h)
        for which in range(2):
            for slot in slots:
                if_used(slot, lambda slot=slot, which=which: halo_arrival(which, h, slot).wait_recv())
        keys = store[0, h].reshape(padded * block, HD)
        values = store[1, h].reshape(padded * block, HD)
        mixed = []
        for b in range(blocks):
            scores = lax.dot_general(
                query[b * block : (b + 1) * block],
                keys,
                (((1,), (1,)), ((), ())),
                preferred_element_type=jnp.float32,
            )
            scores = scores * scale + bias_ref[b : b + 1, :]
            peak = jnp.max(scores, axis=1, keepdims=True)
            weights = jnp.exp(scores - peak)
            denominator = jnp.sum(weights, axis=1, keepdims=True)
            total = jnp.dot(
                weights.astype(jnp.bfloat16), values, preferred_element_type=jnp.float32
            )
            mixed.append(total / denominator)
        mixed = jnp.concatenate(mixed, axis=0)
        first = mixed.astype(jnp.bfloat16)
        rest = mixed - first.astype(jnp.float32)
        second = rest.astype(jnp.bfloat16)
        third = (rest - second.astype(jnp.float32)).astype(jnp.bfloat16)
        sign = sign_ref[...]
        turned = jnp.dot(first, sign, preferred_element_type=jnp.float32)
        turned = turned + jnp.dot(second, sign, preferred_element_type=jnp.float32)
        turned = turned + jnp.dot(third, sign, preferred_element_type=jnp.float32)
        turned = turned * scale
        for b in range(blocks):
            live = position < tokens_ref[me * blocks + b]
            result = jnp.where(live, turned[b * block : (b + 1) * block], 0.0)
            for owner in range(count_head):
                staged[h, owner, b] = result[owner * part : (owner + 1) * part].astype(jnp.bfloat16)
        for offset in range(1, count_head):
            back_copy(offset, h).start()
        back_own(h).start()
        return carry

    lax.fori_loop(0, heads, attend, 0)

    def finish(h, carry):
        for which in range(3):
            for offset in range(1, count_head):
                head_copy(which, offset, h).wait_send()
        for which in range(2):
            for slot in slots:
                if_used(slot, lambda slot=slot, which=which: halo_copy(which, h, slot).wait_send())
        for offset in range(1, count_head):
            back_copy(offset, h).wait()
        back_own(h).wait()
        return carry

    lax.fori_loop(0, heads, finish, 0)


def shards(query_rows, key_rows, value_rows, pair_list, block_tokens):
    count_head = lax.axis_size("head")
    count_tm = lax.axis_size("tm")
    blocks, part, full_width = query_rows.shape
    block = part * count_head
    heads = full_width // (HD * count_head)
    total_blocks, listed = pair_list.shape
    slots = incoming_slots(count_tm)
    filled = blocks + len(slots)
    per_lane_tile = max(1, LANES // block)
    padded = -(-filled // per_lane_tile) * per_lane_tile
    shard_rows = -(-count_tm // 8) * 8
    sizes = (count_head, count_tm, blocks, part, heads, block, total_blocks, slots, padded)
    peers = max(1, count_head - 1)
    in_hbm = pl.BlockSpec(memory_space=pltpu.HBM)
    dma = pltpu.SemaphoreType.DMA
    return pl.pallas_call(
        functools.partial(kernel, sizes),
        out_shape=jax.ShapeDtypeStruct(query_rows.shape, jnp.bfloat16),
        in_specs=[in_hbm] * 5,
        out_specs=in_hbm,
        scratch_shapes=[
            pltpu.VMEM((3, heads, count_head, blocks, part, HD), jnp.bfloat16),
            pltpu.VMEM((2, heads, padded, block, HD), jnp.bfloat16),
            pltpu.VMEM((2, heads, len(slots), block, HD), jnp.bfloat16),
            pltpu.VMEM((heads, count_head, blocks, part, HD), jnp.bfloat16),
            pltpu.VMEM((total_blocks, listed), jnp.int32),
            pltpu.SMEM((total_blocks,), jnp.int32),
            pltpu.VMEM((count_tm, blocks, LANES), jnp.float32),
            pltpu.VMEM((NEAR_CAP, count_tm, 1, LANES), jnp.float32),
            pltpu.VMEM((shard_rows, LANES), jnp.float32),
            pltpu.VMEM((blocks, padded * block), jnp.float32),
            pltpu.VMEM((HD, HD), jnp.bfloat16),
            dma((3, peers, heads)),
            dma((3, peers, heads)),
            dma((3, heads)),
            dma((2, heads, len(slots))),
            dma((2, heads, len(slots))),
            dma((peers, heads)),
            dma((peers, heads)),
            dma((heads,)),
            dma(()),
            dma(()),
        ],
        compiler_params=pltpu.CompilerParams(
            collective_id=0, has_side_effects=True, vmem_limit_bytes=67_043_328
        ),
    )(query_rows, key_rows, value_rows, pair_list, block_tokens)


def solution(mesh):
    placed = (
        P(("grp", "tm"), "head", None),
        P(("grp", "tm"), "head", None),
        P(("grp", "tm"), "head", None),
        P("grp", None),
        P("grp"),
    )
    return jax.shard_map(
        shards,
        mesh=mesh,
        in_specs=placed,
        out_specs=P(("grp", "tm"), "head", None),
        check_vma=False,
    )
```

```python
import functools
import math

import jax
import jax.numpy as jnp
from jax import lax
from jax.experimental import pallas as pl
from jax.experimental.pallas import tpu as pltpu
from jax.sharding import PartitionSpec as P

HD = 128
NEAR_CAP = 2
FAR_CAP = 1
LANES = 128
MESH = pl.DeviceIdType.MESH


def incoming_slots(count_tm):
    slots = []
    for offset in range(1, count_tm):
        capacity = NEAR_CAP if offset in (1, count_tm - 1) else FAR_CAP
        slots += [(offset, place) for place in range(capacity)]
    return slots


def sign_table(dimension):
    rows = lax.broadcasted_iota(jnp.int32, (dimension, dimension), 0)
    columns = lax.broadcasted_iota(jnp.int32, (dimension, dimension), 1)
    common = rows & columns
    parity = jnp.zeros((dimension, dimension), jnp.int32)
    for bit_level in range(dimension.bit_length() - 1):
        parity = parity + ((common >> bit_level) & 1)
    return jnp.where((parity & 1) == 0, 1.0, -1.0).astype(jnp.float32)


def kernel(
    sizes,
    query_ref,
    key_ref,
    value_ref,
    pair_ref,
    tokens_far,
    out_ref,
    gathered,
    store,
    outbox,
    staged,
    pair_here,
    tokens_ref,
    listed_ref,
    place_ref,
    wanted_ref,
    bias_ref,
    sign_ref,
    head_send,
    head_recv,
    local_sem,
    halo_send,
    halo_recv,
    back_send,
    back_recv,
    back_local,
    pair_sem,
    tokens_sem,
):
    count_head, count_tm, blocks, part, heads, block, total_blocks, slots, padded = sizes
    width = heads * HD
    my_head = lax.axis_index("head")
    me = lax.axis_index("tm")
    scale = 1.0 / math.sqrt(HD)
    slot_of = {slot: i for i, slot in enumerate(slots)}
    sources = (key_ref, value_ref, query_ref)

    for offset in range(1, count_head):
        peer = lax.rem(my_head + offset, count_head)
        pl.semaphore_signal(
            pltpu.get_barrier_semaphore(), inc=1, device_id={"head": peer}, device_id_type=MESH
        )

    def columns_of(owner, h):
        return pl.ds(pl.multiple_of(owner * width + h * HD, HD), HD)

    def head_copy(which, offset, h):
        peer = lax.rem(my_head + offset, count_head)
        return pltpu.make_async_remote_copy(
            src_ref=sources[which].at[:, :, columns_of(peer, h)],
            dst_ref=gathered.at[which, h, my_head],
            send_sem=head_send.at[which, offset - 1, h],
            recv_sem=head_recv.at[which, offset - 1, h],
            device_id={"head": peer},
            device_id_type=MESH,
        )

    def local_copy(which, h):
        return pltpu.make_async_copy(
            sources[which].at[:, :, columns_of(my_head, h)],
            gathered.at[which, h, my_head],
            local_sem.at[which, h],
        )

    def halo_copy(which, h, slot):
        offset, place = slot
        peer = lax.rem(me + offset, count_tm)
        landing = slot_of[(count_tm - offset, place)]
        return pltpu.make_async_remote_copy(
            src_ref=outbox.at[which, h, slot_of[slot]],
            dst_ref=store.at[which, h, blocks + landing],
            send_sem=halo_send.at[which, h, slot_of[slot]],
            recv_sem=halo_recv.at[which, h, landing],
            device_id={"tm": peer},
            device_id_type=MESH,
        )

    def halo_arrival(which, h, slot):
        i = slot_of[slot]
        peer = lax.rem(me + slot[0], count_tm)
        return pltpu.make_async_remote_copy(
            src_ref=outbox.at[which, h, i],
            dst_ref=store.at[which, h, blocks + i],
            send_sem=halo_send.at[which, h, i],
            recv_sem=halo_recv.at[which, h, i],
            device_id={"tm": peer},
            device_id_type=MESH,
        )

    def if_used(slot, action):
        if slot[1] < FAR_CAP:
            action()
        else:
            peer = lax.rem(me + slot[0], count_tm)
            near = (peer == me + 1) | (peer == me - 1)
            pl.when(near)(action)

    def back_copy(offset, h):
        peer = lax.rem(my_head + offset, count_head)
        return pltpu.make_async_remote_copy(
            src_ref=staged.at[h, peer],
            dst_ref=out_ref.at[:, :, columns_of(my_head, h)],
            send_sem=back_send.at[offset - 1, h],
            recv_sem=back_recv.at[offset - 1, h],
            device_id={"head": peer},
            device_id_type=MESH,
        )

    def back_own(h):
        return pltpu.make_async_copy(
            staged.at[h, my_head],
            out_ref.at[:, :, columns_of(my_head, h)],
            back_local.at[h],
        )

    store[:, :, blocks:] = jnp.zeros((2, heads, padded - blocks, block, HD), jnp.bfloat16)
    for offset in range(1, count_tm):
        peer = lax.rem(me + offset, count_tm)
        pl.semaphore_signal(
            pltpu.get_barrier_semaphore(), inc=1, device_id={"tm": peer}, device_id_type=MESH
        )
    pair_copy = pltpu.make_async_copy(pair_ref, pair_here, pair_sem)
    pair_copy.start()
    tokens_copy = pltpu.make_async_copy(tokens_far, tokens_ref, tokens_sem)
    tokens_copy.start()

    def start_local(h, carry):
        for which in range(3):
            local_copy(which, h).start()
        return carry

    lax.fori_loop(0, heads, start_local, 0)
    sign_ref[...] = sign_table(HD).astype(jnp.bfloat16)
    pl.semaphore_wait(pltpu.get_barrier_semaphore(), count_head - 1 + count_tm - 1)

    def start_remote(h, carry):
        for which in range(3):
            for offset in range(1, count_head):
                head_copy(which, offset, h).start()
        return carry

    lax.fori_loop(0, heads, start_remote, 0)

    pair_copy.wait()
    tokens_copy.wait()
    pairs = pair_here[...]
    lane = lax.broadcasted_iota(jnp.int32, (1, LANES), 1)
    listed = jnp.zeros((total_blocks, LANES), jnp.float32)
    token_row = jnp.zeros((1, LANES), jnp.float32)
    for k in range(total_blocks):
        found = jnp.max(jnp.where(pairs == k, 1.0, 0.0), axis=1, keepdims=True)
        here = jnp.where(lane == k, 1.0, 0.0)
        listed = listed + found * here
        token_row = token_row + here * tokens_ref[k].astype(jnp.float32)
    wanted_ref[...] = jnp.zeros_like(wanted_ref)
    for t in range(count_tm):
        of_shard = listed[t * blocks : (t + 1) * blocks]
        listed_ref[t] = of_shard
        wanted_ref[t : t + 1, :] = jnp.max(of_shard, axis=0, keepdims=True)
    low = lax.broadcasted_iota(jnp.int32, (LANES, LANES), 0)
    high = lax.broadcasted_iota(jnp.int32, (LANES, LANES), 1)
    low_shard, high_shard = jnp.zeros_like(low), jnp.zeros_like(high)
    lane_shard = jnp.zeros_like(lane)
    for t in range(1, count_tm):
        low_shard = low_shard + jnp.where(low >= t * blocks, 1, 0)
        high_shard = high_shard + jnp.where(high >= t * blocks, 1, 0)
        lane_shard = lane_shard + jnp.where(lane >= t * blocks, 1, 0)
    before = jnp.where((low_shard == high_shard) & (low < high), 1.0, 0.0).astype(jnp.bfloat16)
    wanted = wanted_ref[...]
    rank = jnp.dot(wanted.astype(jnp.bfloat16), before, preferred_element_type=jnp.float32)
    for place in range(NEAR_CAP):
        chosen = jnp.where(rank == float(place), wanted, 0.0)
        for t in range(count_tm):
            place_ref[place, t] = chosen[t : t + 1, :]
    picks = []
    for offset, place in slots:
        row = place_ref[place, lax.rem(me + offset, count_tm)]
        picks.append(
            [
                jnp.sum(jnp.where(lane == me * blocks + j, row, 0.0), axis=1, keepdims=True)
                for j in range(blocks)
            ]
        )
    mine = listed_ref[me]
    key_lane = lax.broadcasted_iota(jnp.int32, (1, padded * block), 1)
    key_end = jnp.zeros((blocks, padded * block), jnp.float32)
    for i in range(blocks + len(slots)):
        if i < blocks:
            kept_tokens = jnp.where(lane == me * blocks + i, token_row, 0.0)
        else:
            offset, place = slots[i - blocks]
            owner = lax.rem(me + offset, count_tm)
            row = place_ref[place, me]
            kept_tokens = jnp.where(lane_shard == owner, row * token_row, 0.0)
        kept = jnp.sum(mine * kept_tokens, axis=1, keepdims=True)
        inside = jnp.where((key_lane >= i * block) & (key_lane < (i + 1) * block), 1.0, 0.0)
        key_end = key_end + inside * (kept + float(i * block))
    bias_ref[...] = jnp.where(key_lane.astype(jnp.float32) < key_end, 0.0, -1e30)

    def arrived(which, h):
        local_copy(which, h).wait()
        for offset in range(1, count_head):
            head_copy(which, offset, h).wait_recv()
        rows = jnp.concatenate(
            [
                gathered[which, h, :, b].astype(jnp.float32).reshape(block, HD)
                for b in range(blocks)
            ],
            axis=0,
        ).astype(jnp.bfloat16)
        turned = jnp.dot(rows, sign_ref[...], preferred_element_type=jnp.float32) * scale
        return turned.astype(jnp.bfloat16)

    def spread(h):
        for which in range(2):
            turned = arrived(which, h)
            store[which, h, 0:blocks] = turned.reshape(blocks, block, HD)
            wide = turned.astype(jnp.float32)
            for i, slot in enumerate(slots):
                sent = picks[i][0] * wide[0:block]
                for j in range(1, blocks):
                    sent = sent + picks[i][j] * wide[j * block : (j + 1) * block]
                outbox[which, h, i] = sent.astype(jnp.bfloat16)
            for slot in slots:
                if_used(slot, lambda slot=slot, which=which: halo_copy(which, h, slot).start())

    position = lax.broadcasted_iota(jnp.int32, (block, HD), 0)

    def attend(h):
        query = arrived(2, h)
        for which in range(2):
            for slot in slots:
                if_used(slot, lambda slot=slot, which=which: halo_arrival(which, h, slot).wait_recv())
        keys = store[0, h].reshape(padded * block, HD)
        values = store[1, h].reshape(padded * block, HD)
        mixed = []
        for b in range(blocks):
            scores = lax.dot_general(
                query[b * block : (b + 1) * block],
                keys,
                (((1,), (1,)), ((), ())),
                preferred_element_type=jnp.float32,
            )
            scores = scores * scale + bias_ref[b : b + 1, :]
            peak = jnp.max(scores, axis=1, keepdims=True)
            weights = jnp.exp(scores - peak)
            denominator = jnp.sum(weights, axis=1, keepdims=True)
            total = jnp.dot(
                weights.astype(jnp.bfloat16), values, preferred_element_type=jnp.float32
            )
            mixed.append(total / denominator)
        mixed = jnp.concatenate(mixed, axis=0)
        first = mixed.astype(jnp.bfloat16)
        rest = mixed - first.astype(jnp.float32)
        second = rest.astype(jnp.bfloat16)
        third = (rest - second.astype(jnp.float32)).astype(jnp.bfloat16)
        sign = sign_ref[...]
        turned = jnp.dot(first, sign, preferred_element_type=jnp.float32)
        turned = turned + jnp.dot(second, sign, preferred_element_type=jnp.float32)
        turned = turned + jnp.dot(third, sign, preferred_element_type=jnp.float32)
        turned = turned * scale
        for b in range(blocks):
            live = position < tokens_ref[me * blocks + b]
            result = jnp.where(live, turned[b * block : (b + 1) * block], 0.0)
            for owner in range(count_head):
                staged[h, owner, b] = result[owner * part : (owner + 1) * part].astype(jnp.bfloat16)
        for offset in range(1, count_head):
            back_copy(offset, h).start()
        back_own(h).start()

    def step(h, carry):
        pl.when(h < heads)(lambda: spread(h))
        pl.when(h >= 1)(lambda: attend(h - 1))
        return carry

    lax.fori_loop(0, heads + 1, step, 0)

    def finish(h, carry):
        for which in range(3):
            for offset in range(1, count_head):
                head_copy(which, offset, h).wait_send()
        for which in range(2):
            for slot in slots:
                if_used(slot, lambda slot=slot, which=which: halo_copy(which, h, slot).wait_send())
        for offset in range(1, count_head):
            back_copy(offset, h).wait()
        back_own(h).wait()
        return carry

    lax.fori_loop(0, heads, finish, 0)


def shards(query_rows, key_rows, value_rows, pair_list, block_tokens):
    count_head = lax.axis_size("head")
    count_tm = lax.axis_size("tm")
    blocks, part, full_width = query_rows.shape
    block = part * count_head
    heads = full_width // (HD * count_head)
    total_blocks, listed = pair_list.shape
    slots = incoming_slots(count_tm)
    filled = blocks + len(slots)
    per_lane_tile = max(1, LANES // block)
    padded = -(-filled // per_lane_tile) * per_lane_tile
    shard_rows = -(-count_tm // 8) * 8
    sizes = (count_head, count_tm, blocks, part, heads, block, total_blocks, slots, padded)
    peers = max(1, count_head - 1)
    in_hbm = pl.BlockSpec(memory_space=pltpu.HBM)
    dma = pltpu.SemaphoreType.DMA
    return pl.pallas_call(
        functools.partial(kernel, sizes),
        out_shape=jax.ShapeDtypeStruct(query_rows.shape, jnp.bfloat16),
        in_specs=[in_hbm] * 5,
        out_specs=in_hbm,
        scratch_shapes=[
            pltpu.VMEM((3, heads, count_head, blocks, part, HD), jnp.bfloat16),
            pltpu.VMEM((2, heads, padded, block, HD), jnp.bfloat16),
            pltpu.VMEM((2, heads, len(slots), block, HD), jnp.bfloat16),
            pltpu.VMEM((heads, count_head, blocks, part, HD), jnp.bfloat16),
            pltpu.VMEM((total_blocks, listed), jnp.int32),
            pltpu.SMEM((total_blocks,), jnp.int32),
            pltpu.VMEM((count_tm, blocks, LANES), jnp.float32),
            pltpu.VMEM((NEAR_CAP, count_tm, 1, LANES), jnp.float32),
            pltpu.VMEM((shard_rows, LANES), jnp.float32),
            pltpu.VMEM((blocks, padded * block), jnp.float32),
            pltpu.VMEM((HD, HD), jnp.bfloat16),
            dma((3, peers, heads)),
            dma((3, peers, heads)),
            dma((3, heads)),
            dma((2, heads, len(slots))),
            dma((2, heads, len(slots))),
            dma((peers, heads)),
            dma((peers, heads)),
            dma((heads,)),
            dma(()),
            dma(()),
        ],
        compiler_params=pltpu.CompilerParams(
            collective_id=0, has_side_effects=True, vmem_limit_bytes=32 * 1024 * 1024
        ),
    )(*[pltpu.with_memory_space_constraint(x, pltpu.HBM) for x in (query_rows, key_rows, value_rows, pair_list, block_tokens)])


def solution(mesh):
    placed = (
        P(("grp", "tm"), "head", None),
        P(("grp", "tm"), "head", None),
        P(("grp", "tm"), "head", None),
        P("grp", None),
        P("grp"),
    )
    return jax.shard_map(
        shards,
        mesh=mesh,
        in_specs=placed,
        out_specs=P(("grp", "tm"), "head", None),
        check_vma=False,
    )
```

```python
import functools
import math

import jax
import jax.numpy as jnp
from jax import lax
from jax.experimental import pallas as pl
from jax.experimental.pallas import tpu as pltpu
from jax.sharding import PartitionSpec as P

HD = 128
NEAR_CAP = 2
FAR_CAP = 1
LANES = 128
MESH = pl.DeviceIdType.MESH


def incoming_slots(count_tm):
    slots = []
    for offset in range(1, count_tm):
        capacity = NEAR_CAP if offset in (1, count_tm - 1) else FAR_CAP
        slots += [(offset, place) for place in range(capacity)]
    return slots


def sign_table(dimension):
    rows = lax.broadcasted_iota(jnp.int32, (dimension, dimension), 0)
    columns = lax.broadcasted_iota(jnp.int32, (dimension, dimension), 1)
    common = rows & columns
    parity = jnp.zeros((dimension, dimension), jnp.int32)
    for bit_level in range(dimension.bit_length() - 1):
        parity = parity + ((common >> bit_level) & 1)
    return jnp.where((parity & 1) == 0, 1.0, -1.0).astype(jnp.float32)


def kernel(
    sizes,
    query_ref,
    key_ref,
    value_ref,
    pair_ref,
    tokens_far,
    out_ref,
    gathered,
    store,
    outbox,
    staged,
    pair_here,
    tokens_ref,
    listed_ref,
    place_ref,
    wanted_ref,
    bias_ref,
    sign_ref,
    head_send,
    head_recv,
    local_sem,
    halo_send,
    halo_recv,
    back_send,
    back_recv,
    back_local,
    pair_sem,
    tokens_sem,
):
    count_head, count_tm, blocks, part, heads, block, total_blocks, slots, padded = sizes
    width = heads * HD
    my_head = lax.axis_index("head")
    me = lax.axis_index("tm")
    scale = 1.0 / math.sqrt(HD)
    slot_of = {slot: i for i, slot in enumerate(slots)}
    sources = (key_ref, value_ref, query_ref)

    for offset in range(1, count_head):
        peer = lax.rem(my_head + offset, count_head)
        pl.semaphore_signal(
            pltpu.get_barrier_semaphore(), inc=1, device_id={"head": peer}, device_id_type=MESH
        )

    def columns_of(owner, h):
        return pl.ds(pl.multiple_of(owner * width + h * HD, HD), HD)

    def head_copy(which, offset, h):
        peer = lax.rem(my_head + offset, count_head)
        return pltpu.make_async_remote_copy(
            src_ref=sources[which].at[:, :, columns_of(peer, h)],
            dst_ref=gathered.at[which, h, my_head],
            send_sem=head_send.at[which, offset - 1, h],
            recv_sem=head_recv.at[which, offset - 1, h],
            device_id={"head": peer},
            device_id_type=MESH,
        )

    def local_copy(which, h):
        return pltpu.make_async_copy(
            sources[which].at[:, :, columns_of(my_head, h)],
            gathered.at[which, h, my_head],
            local_sem.at[which, h],
        )

    def halo_copy(which, h, slot):
        offset, place = slot
        peer = lax.rem(me + offset, count_tm)
        landing = slot_of[(count_tm - offset, place)]
        return pltpu.make_async_remote_copy(
            src_ref=outbox.at[which, h, slot_of[slot]],
            dst_ref=store.at[which, h, blocks + landing],
            send_sem=halo_send.at[which, h, slot_of[slot]],
            recv_sem=halo_recv.at[which, h, landing],
            device_id={"tm": peer},
            device_id_type=MESH,
        )

    def halo_arrival(which, h, slot):
        i = slot_of[slot]
        peer = lax.rem(me + slot[0], count_tm)
        return pltpu.make_async_remote_copy(
            src_ref=outbox.at[which, h, i],
            dst_ref=store.at[which, h, blocks + i],
            send_sem=halo_send.at[which, h, i],
            recv_sem=halo_recv.at[which, h, i],
            device_id={"tm": peer},
            device_id_type=MESH,
        )

    def if_used(slot, action):
        if slot[1] < FAR_CAP:
            action()
        else:
            peer = lax.rem(me + slot[0], count_tm)
            near = (peer == me + 1) | (peer == me - 1)
            pl.when(near)(action)

    def back_copy(offset, h):
        peer = lax.rem(my_head + offset, count_head)
        return pltpu.make_async_remote_copy(
            src_ref=staged.at[h, peer],
            dst_ref=out_ref.at[:, :, columns_of(my_head, h)],
            send_sem=back_send.at[offset - 1, h],
            recv_sem=back_recv.at[offset - 1, h],
            device_id={"head": peer},
            device_id_type=MESH,
        )

    def back_own(h):
        return pltpu.make_async_copy(
            staged.at[h, my_head],
            out_ref.at[:, :, columns_of(my_head, h)],
            back_local.at[h],
        )

    store[:, :, blocks:] = jnp.zeros((2, heads, padded - blocks, block, HD), jnp.bfloat16)
    for offset in range(1, count_tm):
        peer = lax.rem(me + offset, count_tm)
        pl.semaphore_signal(
            pltpu.get_barrier_semaphore(), inc=1, device_id={"tm": peer}, device_id_type=MESH
        )
    pair_copy = pltpu.make_async_copy(pair_ref, pair_here, pair_sem)
    pair_copy.start()
    tokens_copy = pltpu.make_async_copy(tokens_far, tokens_ref, tokens_sem)
    tokens_copy.start()

    def start_local(h, carry):
        for which in range(3):
            local_copy(which, h).start()
        return carry

    lax.fori_loop(0, heads, start_local, 0)
    sign_ref[...] = sign_table(HD).astype(jnp.bfloat16)
    pl.semaphore_wait(pltpu.get_barrier_semaphore(), count_head - 1 + count_tm - 1)

    def start_remote(which, h):
        for offset in range(1, count_head):
            head_copy(which, offset, h).start()

    def start_step(h, carry):
        @pl.when(h < heads)
        def _():
            start_remote(0, h)
            start_remote(1, h)

        pl.when(h >= 1)(lambda: start_remote(2, h - 1))
        return carry

    lax.fori_loop(0, heads + 1, start_step, 0)

    pair_copy.wait()
    tokens_copy.wait()
    pairs = pair_here[...]
    lane = lax.broadcasted_iota(jnp.int32, (1, LANES), 1)
    listed = jnp.zeros((total_blocks, LANES), jnp.float32)
    token_row = jnp.zeros((1, LANES), jnp.float32)
    for k in range(total_blocks):
        found = jnp.max(jnp.where(pairs == k, 1.0, 0.0), axis=1, keepdims=True)
        here = jnp.where(lane == k, 1.0, 0.0)
        listed = listed + found * here
        token_row = token_row + here * tokens_ref[k].astype(jnp.float32)
    wanted_ref[...] = jnp.zeros_like(wanted_ref)
    for t in range(count_tm):
        of_shard = listed[t * blocks : (t + 1) * blocks]
        listed_ref[t] = of_shard
        wanted_ref[t : t + 1, :] = jnp.max(of_shard, axis=0, keepdims=True)
    low = lax.broadcasted_iota(jnp.int32, (LANES, LANES), 0)
    high = lax.broadcasted_iota(jnp.int32, (LANES, LANES), 1)
    low_shard, high_shard = jnp.zeros_like(low), jnp.zeros_like(high)
    lane_shard = jnp.zeros_like(lane)
    for t in range(1, count_tm):
        low_shard = low_shard + jnp.where(low >= t * blocks, 1, 0)
        high_shard = high_shard + jnp.where(high >= t * blocks, 1, 0)
        lane_shard = lane_shard + jnp.where(lane >= t * blocks, 1, 0)
    before = jnp.where((low_shard == high_shard) & (low < high), 1.0, 0.0).astype(jnp.bfloat16)
    wanted = wanted_ref[...]
    rank = jnp.dot(wanted.astype(jnp.bfloat16), before, preferred_element_type=jnp.float32)
    for place in range(NEAR_CAP):
        chosen = jnp.where(rank == float(place), wanted, 0.0)
        for t in range(count_tm):
            place_ref[place, t] = chosen[t : t + 1, :]
    picks = []
    for offset, place in slots:
        row = place_ref[place, lax.rem(me + offset, count_tm)]
        picks.append(
            [
                jnp.sum(jnp.where(lane == me * blocks + j, row, 0.0), axis=1, keepdims=True)
                for j in range(blocks)
            ]
        )
    mine = listed_ref[me]
    key_lane = lax.broadcasted_iota(jnp.int32, (1, padded * block), 1)
    key_end = jnp.zeros((blocks, padded * block), jnp.float32)
    for i in range(blocks + len(slots)):
        if i < blocks:
            kept_tokens = jnp.where(lane == me * blocks + i, token_row, 0.0)
        else:
            offset, place = slots[i - blocks]
            owner = lax.rem(me + offset, count_tm)
            row = place_ref[place, me]
            kept_tokens = jnp.where(lane_shard == owner, row * token_row, 0.0)
        kept = jnp.sum(mine * kept_tokens, axis=1, keepdims=True)
        inside = jnp.where((key_lane >= i * block) & (key_lane < (i + 1) * block), 1.0, 0.0)
        key_end = key_end + inside * (kept + float(i * block))
    bias_ref[...] = jnp.where(key_lane.astype(jnp.float32) < key_end, 0.0, -1e30)

    def arrived(which, h):
        local_copy(which, h).wait()
        for offset in range(1, count_head):
            head_copy(which, offset, h).wait_recv()
        rows = jnp.concatenate(
            [
                gathered[which, h, :, b].astype(jnp.float32).reshape(block, HD)
                for b in range(blocks)
            ],
            axis=0,
        ).astype(jnp.bfloat16)
        turned = jnp.dot(rows, sign_ref[...], preferred_element_type=jnp.float32) * scale
        return turned.astype(jnp.bfloat16)

    def spread(h):
        for which in range(2):
            turned = arrived(which, h)
            store[which, h, 0:blocks] = turned.reshape(blocks, block, HD)
            wide = turned.astype(jnp.float32)
            for i, slot in enumerate(slots):
                sent = picks[i][0] * wide[0:block]
                for j in range(1, blocks):
                    sent = sent + picks[i][j] * wide[j * block : (j + 1) * block]
                outbox[which, h, i] = sent.astype(jnp.bfloat16)
            for slot in slots:
                if_used(slot, lambda slot=slot, which=which: halo_copy(which, h, slot).start())

    position = lax.broadcasted_iota(jnp.int32, (block, HD), 0)

    def attend(h):
        query = arrived(2, h)
        for which in range(2):
            for slot in slots:
                if_used(slot, lambda slot=slot, which=which: halo_arrival(which, h, slot).wait_recv())
        keys = store[0, h].reshape(padded * block, HD)
        values = store[1, h].reshape(padded * block, HD)
        scores = lax.dot_general(
            query, keys, (((1,), (1,)), ((), ())), preferred_element_type=jnp.float32
        )
        halves, denominators = [], []
        for b in range(blocks):
            of_block = scores[b * block : (b + 1) * block] * scale + bias_ref[b : b + 1, :]
            peak = jnp.max(of_block, axis=1, keepdims=True)
            weights = jnp.exp(of_block - peak)
            denominators.append(jnp.sum(weights, axis=1, keepdims=True))
            halves.append(weights.astype(jnp.bfloat16))
        mixed = jnp.dot(
            jnp.concatenate(halves, axis=0), values, preferred_element_type=jnp.float32
        )
        mixed = mixed / jnp.concatenate(denominators, axis=0)
        first = mixed.astype(jnp.bfloat16)
        rest = mixed - first.astype(jnp.float32)
        second = rest.astype(jnp.bfloat16)
        third = (rest - second.astype(jnp.float32)).astype(jnp.bfloat16)
        sign = sign_ref[...]
        turned = jnp.dot(first, sign, preferred_element_type=jnp.float32)
        turned = turned + jnp.dot(second, sign, preferred_element_type=jnp.float32)
        turned = turned + jnp.dot(third, sign, preferred_element_type=jnp.float32)
        turned = turned * scale
        for b in range(blocks):
            live = position < tokens_ref[me * blocks + b]
            result = jnp.where(live, turned[b * block : (b + 1) * block], 0.0)
            for owner in range(count_head):
                staged[h, owner, b] = result[owner * part : (owner + 1) * part].astype(jnp.bfloat16)
        for offset in range(1, count_head):
            back_copy(offset, h).start()
        back_own(h).start()

    def step(h, carry):
        pl.when(h < heads)(lambda: spread(h))
        pl.when(h >= 1)(lambda: attend(h - 1))
        return carry

    lax.fori_loop(0, heads + 1, step, 0)

    def finish(h, carry):
        for which in range(3):
            for offset in range(1, count_head):
                head_copy(which, offset, h).wait_send()
        for which in range(2):
            for slot in slots:
                if_used(slot, lambda slot=slot, which=which: halo_copy(which, h, slot).wait_send())
        for offset in range(1, count_head):
            back_copy(offset, h).wait()
        back_own(h).wait()
        return carry

    lax.fori_loop(0, heads, finish, 0)


def shards(query_rows, key_rows, value_rows, pair_list, block_tokens):
    count_head = lax.axis_size("head")
    count_tm = lax.axis_size("tm")
    blocks, part, full_width = query_rows.shape
    block = part * count_head
    heads = full_width // (HD * count_head)
    total_blocks, listed = pair_list.shape
    slots = incoming_slots(count_tm)
    filled = blocks + len(slots)
    per_lane_tile = max(1, LANES // block)
    padded = -(-filled // per_lane_tile) * per_lane_tile
    shard_rows = -(-count_tm // 8) * 8
    sizes = (count_head, count_tm, blocks, part, heads, block, total_blocks, slots, padded)
    peers = max(1, count_head - 1)
    in_hbm = pl.BlockSpec(memory_space=pltpu.HBM)
    dma = pltpu.SemaphoreType.DMA
    return pl.pallas_call(
        functools.partial(kernel, sizes),
        out_shape=jax.ShapeDtypeStruct(query_rows.shape, jnp.bfloat16),
        in_specs=[in_hbm] * 5,
        out_specs=in_hbm,
        scratch_shapes=[
            pltpu.VMEM((3, heads, count_head, blocks, part, HD), jnp.bfloat16),
            pltpu.VMEM((2, heads, padded, block, HD), jnp.bfloat16),
            pltpu.VMEM((2, heads, len(slots), block, HD), jnp.bfloat16),
            pltpu.VMEM((heads, count_head, blocks, part, HD), jnp.bfloat16),
            pltpu.VMEM((total_blocks, listed), jnp.int32),
            pltpu.SMEM((total_blocks,), jnp.int32),
            pltpu.VMEM((count_tm, blocks, LANES), jnp.float32),
            pltpu.VMEM((NEAR_CAP, count_tm, 1, LANES), jnp.float32),
            pltpu.VMEM((shard_rows, LANES), jnp.float32),
            pltpu.VMEM((blocks, padded * block), jnp.float32),
            pltpu.VMEM((HD, HD), jnp.bfloat16),
            dma((3, peers, heads)),
            dma((3, peers, heads)),
            dma((3, heads)),
            dma((2, heads, len(slots))),
            dma((2, heads, len(slots))),
            dma((peers, heads)),
            dma((peers, heads)),
            dma((heads,)),
            dma(()),
            dma(()),
        ],
        compiler_params=pltpu.CompilerParams(
            collective_id=0, has_side_effects=True, vmem_limit_bytes=32 * 1024 * 1024
        ),
    )(*[pltpu.with_memory_space_constraint(x, pltpu.HBM) for x in (query_rows, key_rows, value_rows, pair_list, block_tokens)])


def solution(mesh):
    placed = (
        P(("grp", "tm"), "head", None),
        P(("grp", "tm"), "head", None),
        P(("grp", "tm"), "head", None),
        P("grp", None),
        P("grp"),
    )
    return jax.shard_map(
        shards,
        mesh=mesh,
        in_specs=placed,
        out_specs=P(("grp", "tm"), "head", None),
        check_vma=False,
    )
```

```python
import functools
import math

import jax
import jax.numpy as jnp
from jax import lax
from jax.experimental import pallas as pl
from jax.experimental.pallas import tpu as pltpu
from jax.sharding import PartitionSpec as P

HD = 128
NEAR_CAP = 2
FAR_CAP = 1
LANES = 128
LEAD = 2
MESH = pl.DeviceIdType.MESH


def incoming_slots(count_tm):
    slots = []
    for offset in range(1, count_tm):
        capacity = NEAR_CAP if offset in (1, count_tm - 1) else FAR_CAP
        slots += [(offset, place) for place in range(capacity)]
    return slots


def partner(index, offset, count):
    if count & (count - 1):
        return lax.rem(index + offset, count)
    for level in range(count.bit_length() - 1):
        if offset >> level & 1:
            bit = lax.rem(lax.div(index, 1 << level), 2)
            index = index + (1 << level) * (1 - 2 * bit)
    return index


def sign_table(dimension):
    rows = lax.broadcasted_iota(jnp.int32, (dimension, dimension), 0)
    columns = lax.broadcasted_iota(jnp.int32, (dimension, dimension), 1)
    common = rows & columns
    parity = jnp.zeros((dimension, dimension), jnp.int32)
    for bit_level in range(dimension.bit_length() - 1):
        parity = parity + ((common >> bit_level) & 1)
    return jnp.where((parity & 1) == 0, 1.0, -1.0).astype(jnp.float32)


def kernel(
    sizes,
    query_ref,
    key_ref,
    value_ref,
    pair_ref,
    tokens_far,
    out_ref,
    gathered,
    store,
    outbox,
    staged,
    pair_here,
    tokens_ref,
    listed_ref,
    place_ref,
    wanted_ref,
    bias_ref,
    sign_ref,
    head_send,
    head_recv,
    local_sem,
    halo_send,
    halo_recv,
    back_send,
    back_recv,
    back_local,
    pair_sem,
    tokens_sem,
):
    count_head, count_tm, blocks, part, heads, block, total_blocks, slots, padded = sizes
    width = heads * HD
    my_head = lax.axis_index("head")
    me = lax.axis_index("tm")
    scale = 1.0 / math.sqrt(HD)
    slot_of = {slot: i for i, slot in enumerate(slots)}
    sources = (key_ref, value_ref, query_ref)

    for offset in reversed(range(1, count_head)):
        peer = partner(my_head, offset, count_head)
        pl.semaphore_signal(
            pltpu.get_barrier_semaphore(), inc=1, device_id={"head": peer}, device_id_type=MESH
        )

    def columns_of(owner, h):
        return pl.ds(pl.multiple_of(owner * width + h * HD, HD), HD)

    def head_copy(which, offset, h):
        peer = partner(my_head, offset, count_head)
        return pltpu.make_async_remote_copy(
            src_ref=sources[which].at[:, :, columns_of(peer, h)],
            dst_ref=gathered.at[which, h, my_head],
            send_sem=head_send.at[which, offset - 1, h],
            recv_sem=head_recv.at[which, offset - 1, h],
            device_id={"head": peer},
            device_id_type=MESH,
        )

    def local_copy(which, h):
        return pltpu.make_async_copy(
            sources[which].at[:, :, columns_of(my_head, h)],
            gathered.at[which, h, my_head],
            local_sem.at[which, h],
        )

    def halo_copy(which, h, slot):
        offset, place = slot
        peer = lax.rem(me + offset, count_tm)
        landing = slot_of[(count_tm - offset, place)]
        return pltpu.make_async_remote_copy(
            src_ref=outbox.at[which, h, slot_of[slot]],
            dst_ref=store.at[which, h, blocks + landing],
            send_sem=halo_send.at[which, h, slot_of[slot]],
            recv_sem=halo_recv.at[which, h, landing],
            device_id={"tm": peer},
            device_id_type=MESH,
        )

    def halo_arrival(which, h, slot):
        i = slot_of[slot]
        peer = lax.rem(me + slot[0], count_tm)
        return pltpu.make_async_remote_copy(
            src_ref=outbox.at[which, h, i],
            dst_ref=store.at[which, h, blocks + i],
            send_sem=halo_send.at[which, h, i],
            recv_sem=halo_recv.at[which, h, i],
            device_id={"tm": peer},
            device_id_type=MESH,
        )

    def if_used(slot, action):
        if slot[1] < FAR_CAP:
            action()
        else:
            peer = lax.rem(me + slot[0], count_tm)
            near = (peer == me + 1) | (peer == me - 1)
            pl.when(near)(action)

    def back_copy(offset, h):
        peer = partner(my_head, offset, count_head)
        return pltpu.make_async_remote_copy(
            src_ref=staged.at[h, peer],
            dst_ref=out_ref.at[:, :, columns_of(my_head, h)],
            send_sem=back_send.at[offset - 1, h],
            recv_sem=back_recv.at[offset - 1, h],
            device_id={"head": peer},
            device_id_type=MESH,
        )

    def back_own(h):
        return pltpu.make_async_copy(
            staged.at[h, my_head],
            out_ref.at[:, :, columns_of(my_head, h)],
            back_local.at[h],
        )

    store[:, :, blocks:] = jnp.zeros((2, heads, padded - blocks, block, HD), jnp.bfloat16)
    for offset in range(1, count_tm):
        peer = lax.rem(me + offset, count_tm)
        pl.semaphore_signal(
            pltpu.get_barrier_semaphore(), inc=1, device_id={"tm": peer}, device_id_type=MESH
        )
    pair_copy = pltpu.make_async_copy(pair_ref, pair_here, pair_sem)
    pair_copy.start()
    tokens_copy = pltpu.make_async_copy(tokens_far, tokens_ref, tokens_sem)
    tokens_copy.start()

    sign_ref[...] = sign_table(HD).astype(jnp.bfloat16)
    pl.semaphore_wait(pltpu.get_barrier_semaphore(), count_head - 1 + count_tm - 1)

    def start_remote(which, h):
        for offset in reversed(range(1, count_head)):
            head_copy(which, offset, h).start()

    def start_step(h, carry):
        @pl.when(h < heads)
        def _():
            start_remote(0, h)
            start_remote(1, h)

        pl.when(h >= LEAD)(lambda: start_remote(2, h - LEAD))
        return carry

    lax.fori_loop(0, heads + LEAD, start_step, 0)

    def start_local(h, carry):
        for which in range(3):
            local_copy(which, h).start()
        return carry

    lax.fori_loop(0, heads, start_local, 0)

    pair_copy.wait()
    tokens_copy.wait()
    pairs = pair_here[...]
    lane = lax.broadcasted_iota(jnp.int32, (1, LANES), 1)
    listed = jnp.zeros((total_blocks, LANES), jnp.float32)
    token_row = jnp.zeros((1, LANES), jnp.float32)
    for k in range(total_blocks):
        found = jnp.max(jnp.where(pairs == k, 1.0, 0.0), axis=1, keepdims=True)
        here = jnp.where(lane == k, 1.0, 0.0)
        listed = listed + found * here
        token_row = token_row + here * tokens_ref[k].astype(jnp.float32)
    wanted_ref[...] = jnp.zeros_like(wanted_ref)
    for t in range(count_tm):
        of_shard = listed[t * blocks : (t + 1) * blocks]
        listed_ref[t] = of_shard
        wanted_ref[t : t + 1, :] = jnp.max(of_shard, axis=0, keepdims=True)
    low = lax.broadcasted_iota(jnp.int32, (LANES, LANES), 0)
    high = lax.broadcasted_iota(jnp.int32, (LANES, LANES), 1)
    low_shard, high_shard = jnp.zeros_like(low), jnp.zeros_like(high)
    lane_shard = jnp.zeros_like(lane)
    for t in range(1, count_tm):
        low_shard = low_shard + jnp.where(low >= t * blocks, 1, 0)
        high_shard = high_shard + jnp.where(high >= t * blocks, 1, 0)
        lane_shard = lane_shard + jnp.where(lane >= t * blocks, 1, 0)
    before = jnp.where((low_shard == high_shard) & (low < high), 1.0, 0.0).astype(jnp.bfloat16)
    wanted = wanted_ref[...]
    rank = jnp.dot(wanted.astype(jnp.bfloat16), before, preferred_element_type=jnp.float32)
    for place in range(NEAR_CAP):
        chosen = jnp.where(rank == float(place), wanted, 0.0)
        for t in range(count_tm):
            place_ref[place, t] = chosen[t : t + 1, :]
    picks = []
    for offset, place in slots:
        row = place_ref[place, lax.rem(me + offset, count_tm)]
        picks.append(
            [
                jnp.sum(jnp.where(lane == me * blocks + j, row, 0.0), axis=1, keepdims=True)
                for j in range(blocks)
            ]
        )
    mine = listed_ref[me]
    key_lane = lax.broadcasted_iota(jnp.int32, (1, padded * block), 1)
    key_end = jnp.zeros((blocks, padded * block), jnp.float32)
    for i in range(blocks + len(slots)):
        if i < blocks:
            kept_tokens = jnp.where(lane == me * blocks + i, token_row, 0.0)
        else:
            offset, place = slots[i - blocks]
            owner = lax.rem(me + offset, count_tm)
            row = place_ref[place, me]
            kept_tokens = jnp.where(lane_shard == owner, row * token_row, 0.0)
        kept = jnp.sum(mine * kept_tokens, axis=1, keepdims=True)
        inside = jnp.where((key_lane >= i * block) & (key_lane < (i + 1) * block), 1.0, 0.0)
        key_end = key_end + inside * (kept + float(i * block))
    bias_ref[...] = jnp.where(key_lane.astype(jnp.float32) < key_end, 0.0, -1e30)

    def arrived(which, h):
        local_copy(which, h).wait()
        for offset in reversed(range(1, count_head)):
            head_copy(which, offset, h).wait_recv()
        rows = jnp.concatenate(
            [
                gathered[which, h, :, b].astype(jnp.float32).reshape(block, HD)
                for b in range(blocks)
            ],
            axis=0,
        ).astype(jnp.bfloat16)
        turned = jnp.dot(rows, sign_ref[...], preferred_element_type=jnp.float32) * scale
        return turned.astype(jnp.bfloat16)

    def spread(h):
        for which in range(2):
            turned = arrived(which, h)
            store[which, h, 0:blocks] = turned.reshape(blocks, block, HD)
            wide = turned.astype(jnp.float32)
            for i, slot in enumerate(slots):
                sent = picks[i][0] * wide[0:block]
                for j in range(1, blocks):
                    sent = sent + picks[i][j] * wide[j * block : (j + 1) * block]
                outbox[which, h, i] = sent.astype(jnp.bfloat16)
            for slot in slots:
                if_used(slot, lambda slot=slot, which=which: halo_copy(which, h, slot).start())

    position = lax.broadcasted_iota(jnp.int32, (block, HD), 0)

    def attend(h):
        query = arrived(2, h)
        for which in range(2):
            for slot in slots:
                if_used(slot, lambda slot=slot, which=which: halo_arrival(which, h, slot).wait_recv())
        keys = store[0, h].reshape(padded * block, HD)
        values = store[1, h].reshape(padded * block, HD)
        scores = lax.dot_general(
            query, keys, (((1,), (1,)), ((), ())), preferred_element_type=jnp.float32
        )
        halves, denominators = [], []
        for b in range(blocks):
            of_block = scores[b * block : (b + 1) * block] * scale + bias_ref[b : b + 1, :]
            peak = jnp.max(of_block, axis=1, keepdims=True)
            weights = jnp.exp(of_block - peak)
            denominators.append(jnp.sum(weights, axis=1, keepdims=True))
            halves.append(weights.astype(jnp.bfloat16))
        mixed = jnp.dot(
            jnp.concatenate(halves, axis=0), values, preferred_element_type=jnp.float32
        )
        mixed = mixed / jnp.concatenate(denominators, axis=0)
        first = mixed.astype(jnp.bfloat16)
        rest = mixed - first.astype(jnp.float32)
        second = rest.astype(jnp.bfloat16)
        third = (rest - second.astype(jnp.float32)).astype(jnp.bfloat16)
        sign = sign_ref[...]
        turned = jnp.dot(
            jnp.concatenate([first, second], axis=1),
            jnp.concatenate([sign, sign], axis=0),
            preferred_element_type=jnp.float32,
        )
        turned = turned + jnp.dot(third, sign, preferred_element_type=jnp.float32)
        turned = turned * scale
        for b in range(blocks):
            live = position < tokens_ref[me * blocks + b]
            result = jnp.where(live, turned[b * block : (b + 1) * block], 0.0)
            for owner in range(count_head):
                staged[h, owner, b] = result[owner * part : (owner + 1) * part].astype(jnp.bfloat16)
        for offset in reversed(range(1, count_head)):
            back_copy(offset, h).start()
        back_own(h).start()

    def step(h, carry):
        pl.when(h < heads)(lambda: spread(h))
        pl.when(h >= LEAD)(lambda: attend(h - LEAD))
        return carry

    lax.fori_loop(0, heads + LEAD, step, 0)

    def finish(h, carry):
        for which in range(3):
            for offset in reversed(range(1, count_head)):
                head_copy(which, offset, h).wait_send()
        for which in range(2):
            for slot in slots:
                if_used(slot, lambda slot=slot, which=which: halo_copy(which, h, slot).wait_send())
        for offset in reversed(range(1, count_head)):
            back_copy(offset, h).wait()
        back_own(h).wait()
        return carry

    lax.fori_loop(0, heads, finish, 0)


def shards(query_rows, key_rows, value_rows, pair_list, block_tokens):
    count_head = lax.axis_size("head")
    count_tm = lax.axis_size("tm")
    blocks, part, full_width = query_rows.shape
    block = part * count_head
    heads = full_width // (HD * count_head)
    total_blocks, listed = pair_list.shape
    slots = incoming_slots(count_tm)
    filled = blocks + len(slots)
    per_lane_tile = max(1, LANES // block)
    padded = -(-filled // per_lane_tile) * per_lane_tile
    shard_rows = -(-count_tm // 8) * 8
    sizes = (count_head, count_tm, blocks, part, heads, block, total_blocks, slots, padded)
    peers = max(1, count_head - 1)
    in_hbm = pl.BlockSpec(memory_space=pltpu.HBM)
    dma = pltpu.SemaphoreType.DMA
    return pl.pallas_call(
        functools.partial(kernel, sizes),
        out_shape=jax.ShapeDtypeStruct(query_rows.shape, jnp.bfloat16),
        in_specs=[in_hbm] * 5,
        out_specs=in_hbm,
        scratch_shapes=[
            pltpu.VMEM((3, heads, count_head, blocks, part, HD), jnp.bfloat16),
            pltpu.VMEM((2, heads, padded, block, HD), jnp.bfloat16),
            pltpu.VMEM((2, heads, len(slots), block, HD), jnp.bfloat16),
            pltpu.VMEM((heads, count_head, blocks, part, HD), jnp.bfloat16),
            pltpu.VMEM((total_blocks, listed), jnp.int32),
            pltpu.SMEM((total_blocks,), jnp.int32),
            pltpu.VMEM((count_tm, blocks, LANES), jnp.float32),
            pltpu.VMEM((NEAR_CAP, count_tm, 1, LANES), jnp.float32),
            pltpu.VMEM((shard_rows, LANES), jnp.float32),
            pltpu.VMEM((blocks, padded * block), jnp.float32),
            pltpu.VMEM((HD, HD), jnp.bfloat16),
            dma((3, peers, heads)),
            dma((3, peers, heads)),
            dma((3, heads)),
            dma((2, heads, len(slots))),
            dma((2, heads, len(slots))),
            dma((peers, heads)),
            dma((peers, heads)),
            dma((heads,)),
            dma(()),
            dma(()),
        ],
        compiler_params=pltpu.CompilerParams(
            collective_id=0, has_side_effects=True, vmem_limit_bytes=32 * 1024 * 1024
        ),
    )(*[pltpu.with_memory_space_constraint(x, pltpu.HBM) for x in (query_rows, key_rows, value_rows, pair_list, block_tokens)])


def solution(mesh):
    placed = (
        P(("grp", "tm"), "head", None),
        P(("grp", "tm"), "head", None),
        P(("grp", "tm"), "head", None),
        P("grp", None),
        P("grp"),
    )
    return jax.shard_map(
        shards,
        mesh=mesh,
        in_specs=placed,
        out_specs=P(("grp", "tm"), "head", None),
        check_vma=False,
    )
```
